32 devices in a mesh: seq: 8 (over z, x), head: 4 (over y, core).
Axes of the slice: x: 2, y: 2, z: 4, core: 2. Of those that a mesh axis runs over, the one named last changes fastest.
Arguments:
- video_query: bfloat16 [4096, 3072], P(('seq', 'head')), may hold values from -16 to 16
- audio_key: bfloat16 [4096, 3072], P(('seq', 'head')), may hold values from -16 to 16
- audio_value: bfloat16 [4096, 3072], P(('seq', 'head')), may hold values from -6 to 6
- grad_out: bfloat16 [4096, 3072], P(('seq', 'head')), may hold values from -6 to 6
- audio_time: int32 [4096], P(('seq', 'head')), may hold values from -1 to 4999, as said below
Outputs:
- attended: bfloat16 [4096, 3072], P(('seq', 'head'))
- grad_query: bfloat16 [4096, 3072], P(('seq', 'head'))
- grad_key: bfloat16 [4096, 3072], P(('seq', 'head'))
- grad_value: bfloat16 [4096, 3072], P(('seq', 'head'))
The draws below stay inside these ranges and needn't reach their ends.
Inputs may be any that keep to these rules, and one draw needn't show every extreme that they name: `audio_time`: slots r * 512 to (r+1) * 512 - 1 belong to time range r: their live slots come first, with stamps from r * 625 to (r+1) * 625 - 1 in rising order, and the rest hold -1. Every range has at least 170 live slots, and in every draw some range has all 512 live.
All inputs are finite; a program needn't handle non-finite values.
Results may differ from the reference program's by a relative error of at most 0.0061.
Values may be sent and summed in bfloat16 or wider, within the bound.
A program may use at most 192 MiB of HBM per device.

```python
import jax
import jax.numpy as jnp
from jax import lax

D = 3072
HEADS = 24
DH = 128
SHARD_MS = 625
RADIUS_MS = 1000
VSEQ = 512
CAP = 512
NV = 4096
NA = 4096
N_SEQ = 8


def draw_video_query(key, part):
    base = jax.random.normal(jax.random.fold_in(key, 11), (NV, D), jnp.float32)
    base = jnp.clip(base, -6.0, 6.0)
    return base.astype(jnp.bfloat16)


def draw_audio_key(key, part):
    base = jax.random.normal(jax.random.fold_in(key, 21), (NA, D), jnp.float32)
    base = jnp.clip(base, -6.0, 6.0)
    return base.astype(jnp.bfloat16)


def draw_audio_time(key, part):
    range_count = NA // CAP
    counts = jax.random.randint(jax.random.fold_in(key, 31), (range_count,), CAP // 3, CAP + 1)
    busiest = jax.random.randint(jax.random.fold_in(key, 32), (), 0, range_count)
    counts = counts.at[busiest].set(CAP)
    offsets = jax.random.randint(jax.random.fold_in(key, 33), (range_count, CAP), 0, SHARD_MS)
    slot_ids = jnp.arange(CAP, dtype=jnp.int32)[None, :]
    live = slot_ids < counts[:, None]
    ordered = jnp.sort(jnp.where(live, offsets, SHARD_MS + 1), axis=1)
    starts = (jnp.arange(range_count, dtype=jnp.int32) * SHARD_MS)[:, None]
    stamps = jnp.where(live, starts + ordered, -1)
    return stamps.reshape(NA).astype(jnp.int32)


def block_scale(key, shape, split, least, top_value):
    factor_of, own = 1.0, jax.random.fold_in(key, 6)
    for position, parts in split:
        draws = jnp.exp(jax.random.uniform(jax.random.fold_in(own, position), (parts,), jnp.float32, least / len(split), top_value / len(split)))
        factor_of = factor_of * jnp.repeat(draws, shape[position] // parts).reshape([-1 if axis == position else 1 for axis in range(len(shape))])
    return factor_of


def noise(rng, dims, scale, limit, shards=(), kind=jnp.bfloat16):
    loudness = block_scale(rng, dims, shards, -0.22, 0.18) if shards else 1.0
    values = jax.random.normal(rng, dims, jnp.float32) * scale * loudness
    return jnp.minimum(jnp.maximum(values, -limit), limit).astype(kind)


def setup_inputs(seed: int = 0) -> dict:
    splits = jax.random.split(jax.random.key(seed), 6)
    return {
        "video_query": draw_video_query(jax.random.fold_in(splits[5], 71), 0),
        "audio_key": draw_audio_key(jax.random.fold_in(splits[5], 71), 0),
        "audio_value": noise(splits[2], (NA, D), 1.0, 6.0, ((0, 32),)),
        "grad_out": noise(splits[3], (NV, D), 1.0, 6.0, ((0, 32),)),
        "audio_time": draw_audio_time(jax.random.fold_in(splits[5], 71), 0),
    }


NEG_FILL = -1e30


def attend_block(query_rows, key_rows, value_rows, grad_rows, query_stamps, key_stamps):
    scaling = DH ** -0.5
    allowed = (key_stamps[None, :] >= 0) & (jnp.abs(query_stamps[:, None] - key_stamps[None, :]) <= RADIUS_MS)
    query_float = query_rows.astype(jnp.float32)
    key_float = key_rows.astype(jnp.float32)
    value_float = value_rows.astype(jnp.float32)
    grad_float = grad_rows.astype(jnp.float32)
    scores = jnp.einsum("qhd,khd->hqk", query_float, key_float) * scaling
    scores = jnp.where(allowed[None], scores, NEG_FILL)
    row_max = jnp.max(scores, axis=2, keepdims=True)
    row_total = jnp.sum(jnp.exp(scores - row_max), axis=2, keepdims=True)
    log_total = row_max + jnp.log(row_total)
    weights = jnp.exp(scores - log_total)
    weights_low = weights.astype(jnp.bfloat16).astype(jnp.float32)
    attended_full = jnp.einsum("hqk,khd->qhd", weights_low, value_float)
    row_dot = jnp.sum(grad_float * attended_full, axis=2)
    grad_weights = jnp.einsum("qhd,khd->hqk", grad_float, value_float)
    grad_scores = (weights * (grad_weights - row_dot.T[:, :, None])).astype(jnp.bfloat16).astype(jnp.float32)
    grad_query = jnp.einsum("hqk,khd->qhd", grad_scores, key_float) * scaling
    grad_key = jnp.einsum("hqk,qhd->khd", grad_scores, query_float) * scaling
    grad_value = jnp.einsum("hqk,qhd->khd", weights_low, grad_float)
    return attended_full, grad_query, grad_key, grad_value


def reference(video_query, audio_key, audio_value, grad_out, audio_time):
    model_width = video_query.shape[1]
    pad_rows = 2 * CAP
    zero_rows = jnp.zeros((pad_rows, model_width), audio_key.dtype)
    key_padded = jnp.concatenate([zero_rows, audio_key, zero_rows], 0)
    value_padded = jnp.concatenate([zero_rows, audio_value, zero_rows], 0)
    stamp_fill = jnp.full((pad_rows,), -1, jnp.int32)
    stamp_padded = jnp.concatenate([stamp_fill, audio_time.astype(jnp.int32), stamp_fill], 0)
    offsets = (jnp.arange(VSEQ, dtype=jnp.int32) * SHARD_MS) // VSEQ

    def per_range(running, range_index):
        key_sums, value_sums = running
        row_start = (range_index * VSEQ).astype(jnp.int32)
        slot_start = (range_index * CAP).astype(jnp.int32)
        query_rows = lax.dynamic_slice_in_dim(video_query, row_start, VSEQ, 0).reshape(VSEQ, HEADS, DH)
        grad_rows = lax.dynamic_slice_in_dim(grad_out, row_start, VSEQ, 0).reshape(VSEQ, HEADS, DH)
        key_rows = lax.dynamic_slice_in_dim(key_padded, slot_start, 5 * CAP, 0).reshape(5 * CAP, HEADS, DH)
        value_rows = lax.dynamic_slice_in_dim(value_padded, slot_start, 5 * CAP, 0).reshape(5 * CAP, HEADS, DH)
        key_stamps = lax.dynamic_slice_in_dim(stamp_padded, slot_start, 5 * CAP, 0)
        query_stamps = (range_index * SHARD_MS).astype(jnp.int32) + offsets
        attended_full, grad_query, grad_key, grad_value = attend_block(
            query_rows, key_rows, value_rows, grad_rows, query_stamps, key_stamps)
        old_keys = lax.dynamic_slice_in_dim(key_sums, slot_start, 5 * CAP, 0)
        key_sums = lax.dynamic_update_slice_in_dim(key_sums, old_keys + grad_key.reshape(5 * CAP, model_width), slot_start, 0)
        old_values = lax.dynamic_slice_in_dim(value_sums, slot_start, 5 * CAP, 0)
        value_sums = lax.dynamic_update_slice_in_dim(value_sums, old_values + grad_value.reshape(5 * CAP, model_width), slot_start, 0)
        outputs = (attended_full.reshape(VSEQ, model_width).astype(jnp.bfloat16),
                   grad_query.reshape(VSEQ, model_width).astype(jnp.bfloat16))
        return (key_sums, value_sums), outputs

    zero_sums = (jnp.zeros((NA + 4 * CAP, model_width), jnp.float32),
                 jnp.zeros((NA + 4 * CAP, model_width), jnp.float32))
    (key_sums, value_sums), (attended, grad_query) = lax.scan(
        per_range, zero_sums, jnp.arange(N_SEQ, dtype=jnp.int32))
    grad_key = key_sums[pad_rows:pad_rows + NA].astype(jnp.bfloat16)
    grad_value = value_sums[pad_rows:pad_rows + NA].astype(jnp.bfloat16)
    return (attended.reshape(NV, model_width), grad_query.reshape(NV, model_width), grad_key, grad_value)
```

```python
import functools

import jax
import jax.numpy as jnp
from jax import lax
from jax.experimental import pallas as pl
from jax.experimental.pallas import tpu as pltpu
from jax.sharding import PartitionSpec as P

DH = 128
SHARD_MS = 625
RADIUS_MS = 1000
NEG_FILL = -1e30
FAR = 1 << 30
LOG2E = 1.4426950408889634
F32 = jnp.float32
BF16 = jnp.bfloat16
NT = (((1,), (1,)), ((), ()))
NN = (((1,), (0,)), ((), ()))
TN = (((0,), (0,)), ((), ()))


def mm(a, b, dims):
    return lax.dot_general(a, b, dims, preferred_element_type=F32)


def attend_half(half, size, block, q_ref, g_ref, k_ref, v_ref, qt_ref, lo_ref, hi_ref, o_ref,
                dq_ref, dk_acc, dv_acc, s_scr):
    scaling = DH ** (-0.5)

    def q_block(step, carry):
        rows = pl.ds(pl.multiple_of(half * size + step * block, block), block)
        q = q_ref[rows, :]
        g = g_ref[rows, :]
        stamp = qt_ref[rows, :]
        top = jnp.full((block, 1), -jnp.inf, F32)
        for j in range(5):
            cols = slice((half + j) * size, (half + j + 1) * size)
            s = mm(q, k_ref[cols, :], NT)
            if j <= 2:
                allowed = lo_ref[:, cols] >= stamp - RADIUS_MS
            else:
                allowed = hi_ref[:, cols] <= stamp + RADIUS_MS
            s = jnp.where(allowed, s, NEG_FILL)
            s_scr[:, j * size:(j + 1) * size] = s
            top = jnp.maximum(top, jnp.max(s, axis=1, keepdims=True))
        total = jnp.zeros((block, 1), F32)
        for j in range(5):
            here = slice(j * size, (j + 1) * size)
            p = jnp.exp2((s_scr[:, here] - top) * (scaling * LOG2E))
            s_scr[:, here] = p
            total = total + jnp.sum(p, axis=1, keepdims=True)
        inverse = 1.0 / total
        out = jnp.zeros((block, DH), F32)
        for j in range(5):
            here = slice(j * size, (j + 1) * size)
            cols = slice((half + j) * size, (half + j + 1) * size)
            weight = s_scr[:, here] * inverse
            s_scr[:, here] = weight
            low = weight.astype(BF16)
            out = out + mm(low, v_ref[cols, :], NN)
            dv_acc[cols, :] += mm(low, g, TN)
        o_ref[rows, :] = out.astype(BF16)
        row_dot = jnp.sum(g.astype(F32) * out, axis=1, keepdims=True)
        dq = jnp.zeros((block, DH), F32)
        for j in range(5):
            here = slice(j * size, (j + 1) * size)
            cols = slice((half + j) * size, (half + j + 1) * size)
            dp = mm(g, v_ref[cols, :], NT)
            ds = (s_scr[:, here] * (dp - row_dot)).astype(BF16)
            dq = dq + mm(ds, k_ref[cols, :], NN)
            dk_acc[cols, :] += mm(ds, q, TN)
        dq_ref[rows, :] = (dq * scaling).astype(BF16)
        return carry

    lax.fori_loop(0, size // block, q_block, 0)


def whole_kernel(blocks, width, heads, size, block,
                 k_in, v_in, q_in, g_in, t_in,
                 o_out, dq_out, dk_out, dv_out,
                 qt_ref, kwin, vwin, qs, gs, tw, lo, hi, o_st, dq_st, psend, prec, fin, center,
                 dk_acc, dv_acc, s_scr,
                 in_send, in_recv, in_local, t_send, t_recv, t_local,
                 halo_send, halo_recv, th_send, th_recv, part_send, part_recv,
                 out_send, out_recv, out_local):
    scaling = DH ** (-0.5)
    group = 2 * width
    seq = lax.axis_index("seq")
    head = lax.axis_index("head")
    blk = seq // 2
    me = (seq % 2) * width + head
    rows = k_in.shape[0]
    span = 2 * size
    has_low = blk > 0
    has_up = blk < blocks - 1
    mid = pl.ds(span, span)

    def peer(p):
        return (blk * 2 + p // width, p % width)

    low_dev = (seq - 2, head)
    up_dev = (seq + 2, head)

    def remote(src, dst, send, recv, dev):
        return pltpu.make_async_remote_copy(
            src_ref=src, dst_ref=dst, send_sem=send, recv_sem=recv, device_id=dev,
            device_id_type=pl.DeviceIdType.MESH)

    def each_peer(action):
        def step(d, carry):
            action((me + d) % group)
            return carry
        lax.fori_loop(1, group, step, 0)

    def wait_bytes(ref, sem):
        pltpu.make_async_copy(ref, ref, sem).wait()

    barrier = pltpu.get_barrier_semaphore()

    def greet(dev):
        pl.semaphore_signal(barrier, inc=1, device_id=dev, device_id_type=pl.DeviceIdType.MESH)

    each_peer(lambda p: greet(peer(p)))

    @pl.when(has_low)
    def _():
        greet(low_dev)

    @pl.when(has_up)
    def _():
        greet(up_dev)

    pl.semaphore_wait(barrier, group - 1 + has_low.astype(jnp.int32) + has_up.astype(jnp.int32))

    ins = (k_in, v_in, q_in, g_in)

    def landing(a, h, p):
        base = span if a < 2 else 0
        where = pl.ds(pl.multiple_of(base + p * rows, rows), rows)
        return (kwin, vwin, qs, gs)[a].at[h, where]

    def columns(p, h):
        return pl.ds(pl.multiple_of((p * heads + h) * DH, DH), DH)

    def spread(arrays, h):
        for a in arrays:
            pltpu.make_async_copy(ins[a].at[:, columns(me, h)], landing(a, h, me),
                                  in_local.at[a, h]).start()

        def send(p):
            for a in arrays:
                remote(ins[a].at[:, columns(p, h)], landing(a, h, me), in_send.at[a],
                       in_recv.at[a, h], peer(p)).start()
        each_peer(send)

    def arrived(a, h):
        ref = (kwin, vwin, qs, gs)[a]
        wait_bytes(ref.at[h, pl.ds(0, (group - 1) * rows)], in_recv.at[a, h])
        wait_bytes(ref.at[h, pl.ds(0, rows)], in_local.at[a, h])

    pltpu.make_async_copy(t_in, tw.at[group + me], t_local).start()
    each_peer(lambda p: remote(t_in, tw.at[group + me], t_send, t_recv, peer(p)).start())
    def halo_up(a, h):
        ref = (kwin, vwin)[a]
        return remote(ref.at[h, mid], ref.at[h, pl.ds(0, span)], halo_send.at[0, a, h],
                      halo_recv.at[0, a, h], up_dev)

    def halo_down(a, h):
        ref = (kwin, vwin)[a]
        return remote(ref.at[h, mid], ref.at[h, pl.ds(2 * span, span)], halo_send.at[1, a, h],
                      halo_recv.at[1, a, h], low_dev)

    def chunk(part, p):
        return pl.ds(pl.multiple_of(part * span + p * rows, rows), rows)

    def chunk_up(a, h, p, src):
        ref = (kwin, vwin)[a]

        @pl.when(has_up)
        def _():
            remote(src, ref.at[h, chunk(0, p)], halo_send.at[0, a, h], halo_recv.at[0, a, h],
                   up_dev).start()

    def chunk_down(a, h, p, src):
        ref = (kwin, vwin)[a]

        @pl.when(has_low)
        def _():
            remote(src, ref.at[h, chunk(2, p)], halo_send.at[1, a, h], halo_recv.at[1, a, h],
                   low_dev).start()

    def own_halo(h):
        for a in range(2):
            src = ins[a].at[:, columns(me, h)]
            chunk_up(a, h, me, src)
            chunk_down(a, h, me, src)

    spread((0, 1), 0)
    for h in range(heads):
        own_halo(h)
    if heads > 1:
        spread((0, 1), 1)
    for h in range(heads):
        spread((2, 3), h)
        if h + 2 < heads:
            spread((0, 1), h + 2)

    def t_up():
        return remote(tw.at[pl.ds(group, group)], tw.at[pl.ds(0, group)], th_send.at[0],
                      th_recv.at[0], up_dev)

    def t_down():
        return remote(tw.at[pl.ds(group, group)], tw.at[pl.ds(2 * group, group)], th_send.at[1],
                      th_recv.at[1], low_dev)

    def forward(h):
        for a in range(2):
            arrived(a, h)
            ref = (kwin, vwin)[a]

            def pass_on(p, a=a, ref=ref):
                chunk_up(a, h, p, ref.at[h, chunk(1, p)])
                chunk_down(a, h, p, ref.at[h, chunk(1, p)])
            each_peer(pass_on)

    @pl.when(jnp.logical_not(has_low))
    def _():
        kwin[:, 0:span, :] = jnp.zeros((heads, span, DH), BF16)
        vwin[:, 0:span, :] = jnp.zeros((heads, span, DH), BF16)
        tw[0:group] = jnp.full((group, 1, rows), -1, jnp.int32)

    @pl.when(jnp.logical_not(has_up))
    def _():
        kwin[:, 2 * span:3 * span, :] = jnp.zeros((heads, span, DH), BF16)
        vwin[:, 2 * span:3 * span, :] = jnp.zeros((heads, span, DH), BF16)
        tw[2 * group:3 * group] = jnp.full((group, 1, rows), -1, jnp.int32)

    place = lax.broadcasted_iota(jnp.int32, (size, 1), 0)
    offset = lax.div(place * SHARD_MS, jnp.full((size, 1), size, jnp.int32))
    qt_ref[0:size, :] = offset
    qt_ref[size:span, :] = offset + SHARD_MS

    wait_bytes(tw.at[pl.ds(0, group - 1)], t_recv)
    wait_bytes(tw.at[0], t_local)

    @pl.when(has_up)
    def _():
        t_up().start()

    @pl.when(has_low)
    def _():
        t_down().start()

    forward(0)
    if heads > 1:
        forward(1)

    @pl.when(has_low)
    def _():
        t_up().wait_recv()

    @pl.when(has_up)
    def _():
        t_down().wait_recv()

    first = blk * 2 * SHARD_MS
    for i in range(3 * group):
        t = tw[i]
        here = slice(i * rows, (i + 1) * rows)
        lo[:, here] = jnp.where(t >= 0, t - first, -FAR)
        hi[:, here] = jnp.where(t >= 0, t - first, FAR)

    outs = (o_out, dq_out, dk_out, dv_out)

    def piece(p):
        return pl.ds(pl.multiple_of(p * rows, rows), rows)

    def hand_back(i, src, h, p):
        @pl.when(p == me)
        def _():
            pltpu.make_async_copy(src.at[piece(me)], outs[i].at[:, columns(me, h)],
                                  out_local.at[i, h]).start()

        @pl.when(p != me)
        def _():
            remote(src.at[piece(p)], outs[i].at[:, columns(me, h)], out_send.at[i],
                   out_recv.at[i], peer(p)).start()

    def collect(half, h):
        for i, src in enumerate((o_st, dq_st)):
            def step(d, carry, i=i, src=src):
                hand_back(i, src.at[h], h, half * width + (head + d) % width)
                return carry
            lax.fori_loop(0, width, step, 0)

    def part_down(a, h, p):
        return remote(psend.at[0, a, h, piece(p)], prec.at[0, a, h, piece(p)],
                      part_send.at[0, a, h], part_recv.at[0, a, h, p], low_dev)

    def part_up(a, h, p):
        return remote(psend.at[1, a, h, piece(p)], prec.at[1, a, h, piece(p)],
                      part_send.at[1, a, h], part_recv.at[1, a, h, p], up_dev)

    def every_piece(action):
        def step(d, carry):
            action((me + d) % group)
            return carry
        lax.fori_loop(0, group, step, 0)

    def finish(h):
        for a in range(2):
            def one(p, a=a):
                here = piece(p)

                @pl.when(has_up)
                def _():
                    part_down(a, h, p).wait_recv()
                    center[a, h, here] = center[a, h, here] + prec[0, a, h, here].astype(F32)

                @pl.when(has_low)
                def _():
                    part_up(a, h, p).wait_recv()
                    center[a, h, here] = center[a, h, here] + prec[1, a, h, here].astype(F32)

                fin[a, h, here] = center[a, h, here].astype(BF16)
                hand_back(2 + a, fin.at[a, h], h, p)
            every_piece(one)

    def one_head(h, carry):
        for a in range(2):
            @pl.when(has_low)
            def _(a=a):
                halo_up(a, h).wait_recv()

            @pl.when(has_up)
            def _(a=a):
                halo_down(a, h).wait_recv()
        arrived(2, h)
        arrived(3, h)
        dk_acc[...] = jnp.zeros_like(dk_acc)
        dv_acc[...] = jnp.zeros_like(dv_acc)
        refs = (size, block, qs.at[h], gs.at[h], kwin.at[h], vwin.at[h], qt_ref, lo, hi,
                o_st.at[h], dq_st.at[h], dk_acc, dv_acc, s_scr)
        attend_half(0, *refs)
        collect(0, h)

        @pl.when(h + 2 < heads)
        def _():
            forward(h + 2)

        @pl.when(h >= 2)
        def _():
            finish(h - 2)

        attend_half(1, *refs)
        for a, (acc, factor) in enumerate(((dk_acc, scaling), (dv_acc, None))):
            def part(i, acc=acc, factor=factor):
                x = acc[i * span:(i + 1) * span, :]
                return x if factor is None else x * factor

            @pl.when(has_low)
            def _(a=a, part=part):
                psend[0, a, h] = part(0).astype(BF16)
                every_piece(lambda p: part_down(a, h, p).start())

            @pl.when(has_up)
            def _(a=a, part=part):
                psend[1, a, h] = part(2).astype(BF16)
                every_piece(lambda p: part_up(a, h, p).start())

            center[a, h] = part(1)
        collect(1, h)
        return carry

    lax.fori_loop(0, heads, one_head, 0)

    def settle(h, carry):
        finish(h)
        return carry

    lax.fori_loop(max(heads - 2, 0), heads, settle, 0)

    sent = (group - 1) * heads * DH
    wait_bytes(tw.at[pl.ds(0, group - 1)], t_send)
    for a in range(4):
        wait_bytes(ins[a].at[:, pl.ds(0, sent)], in_send.at[a])
        wait_bytes(outs[a].at[:, pl.ds(0, sent)], out_send.at[a])
        wait_bytes(outs[a].at[:, pl.ds(0, sent)], out_recv.at[a])
        for h in range(heads):
            wait_bytes(outs[a].at[:, pl.ds(0, DH)], out_local.at[a, h])

    @pl.when(has_up)
    def _():
        t_up().wait_send()
        for a in range(2):
            for h in range(heads):
                halo_up(a, h).wait_send()
                wait_bytes(psend.at[1, a, h], part_send.at[1, a, h])

    @pl.when(has_low)
    def _():
        t_down().wait_send()
        for a in range(2):
            for h in range(heads):
                halo_down(a, h).wait_send()
                wait_bytes(psend.at[0, a, h], part_send.at[0, a, h])


def hand_over(*refs):
    srcs, dsts, (bufs, in_sem, out_sem) = refs[:4], refs[4:8], refs[8:]
    loads = [pltpu.make_async_copy(srcs[i], bufs.at[i], in_sem.at[i]) for i in range(4)]
    stores = [pltpu.make_async_copy(bufs.at[i], dsts[i], out_sem.at[i]) for i in range(4)]
    for load in loads:
        load.start()
    for load, store in zip(loads, stores):
        load.wait()
        store.start()
    for store in stores:
        store.wait()


def on_device(seq_count, head_count, video_query, audio_key, audio_value, grad_out, audio_time):
    group = 2 * head_count
    rows, features = video_query.shape
    size = rows * head_count
    span = 2 * size
    heads = features // DH // group
    block = min(512, size)
    hbm = pl.BlockSpec(memory_space=pl.ANY)
    dma = pltpu.SemaphoreType.DMA
    pairs = heads * span * 5 * size
    o, dq, dk, dv = pl.pallas_call(
        functools.partial(whole_kernel, seq_count // 2, head_count, heads, size, block),
        in_specs=[hbm] * 5,
        out_specs=[hbm] * 4,
        out_shape=[jax.ShapeDtypeStruct((rows, features), BF16)] * 4,
        scratch_shapes=[
            pltpu.VMEM((span, 1), jnp.int32),
            pltpu.VMEM((heads, 3 * span, DH), BF16),
            pltpu.VMEM((heads, 3 * span, DH), BF16),
            pltpu.VMEM((heads, span, DH), BF16),
            pltpu.VMEM((heads, span, DH), BF16),
            pltpu.VMEM((3 * group, 1, rows), jnp.int32),
            pltpu.VMEM((1, 3 * span), jnp.int32),
            pltpu.VMEM((1, 3 * span), jnp.int32),
            pltpu.VMEM((heads, span, DH), BF16),
            pltpu.VMEM((heads, span, DH), BF16),
            pltpu.VMEM((2, 2, heads, span, DH), BF16),
            pltpu.VMEM((2, 2, heads, span, DH), BF16),
            pltpu.VMEM((2, heads, span, DH), BF16),
            pltpu.VMEM((2, heads, span, DH), F32),
            pltpu.VMEM((3 * span, DH), F32),
            pltpu.VMEM((3 * span, DH), F32),
            pltpu.VMEM((block, 5 * size), F32),
            dma((4,)), dma((4, heads)), dma((4, heads)), dma, dma, dma,
            dma((2, 2, heads)), dma((2, 2, heads)), dma((2,)), dma((2,)),
            dma((2, 2, heads)), dma((2, 2, heads, group)),
            dma((4,)), dma((4,)), dma((4, heads)),
        ],
        compiler_params=pltpu.CompilerParams(
            collective_id=0, has_side_effects=True, vmem_limit_bytes=56 * 1024 * 1024),
        cost_estimate=pl.CostEstimate(flops=12 * pairs * DH, bytes_accessed=16 * rows * features,
                                      transcendentals=pairs),
    )(audio_key, audio_value, video_query, grad_out, audio_time[None, :])
    return pl.pallas_call(
        hand_over, in_specs=[hbm] * 4, out_specs=[hbm] * 4,
        out_shape=[jax.ShapeDtypeStruct((rows, features), BF16)] * 4,
        scratch_shapes=[pltpu.VMEM((4, rows, features), BF16), dma((4,)), dma((4,))],
    )(o, dq, dk, dv)


def solution(mesh):
    rows = P(("seq", "head"), None)
    return jax.shard_map(
        functools.partial(on_device, mesh.shape["seq"], mesh.shape["head"]),
        mesh=mesh,
        in_specs=(rows, rows, rows, rows, P(("seq", "head"))),
        out_specs=(rows, rows, rows, rows),
        check_vma=False,
    )
```

```python
import functools

import jax
import jax.numpy as jnp
from jax import lax
from jax.experimental import pallas as pl
from jax.experimental.pallas import tpu as pltpu
from jax.sharding import PartitionSpec as P

DH = 128
SHARD_MS = 625
RADIUS_MS = 1000
NEG_FILL = -1e30
FAR = 1 << 30
LOG2E = 1.4426950408889634
F32 = jnp.float32
BF16 = jnp.bfloat16
NT = (((1,), (1,)), ((), ()))
NN = (((1,), (0,)), ((), ()))
TN = (((0,), (0,)), ((), ()))


def mm(a, b, dims):
    return lax.dot_general(a, b, dims, preferred_element_type=F32)


def attend_half(half, size, q_ref, g_ref, k_ref, v_ref, qt_ref, lo_ref, hi_ref, o_ref,
                dq_ref, emit, s_scr):
    scaling = DH ** (-0.5)
    rows = slice(half * size, (half + 1) * size)
    q = q_ref[rows, :]
    g = g_ref[rows, :]
    stamp = qt_ref[rows, :]
    top = jnp.full((size, 1), -jnp.inf, F32)
    for j in range(5):
        cols = slice((half + j) * size, (half + j + 1) * size)
        s = mm(q, k_ref[cols, :], NT)
        if j <= 2:
            allowed = lo_ref[:, cols] >= stamp - RADIUS_MS
        else:
            allowed = hi_ref[:, cols] <= stamp + RADIUS_MS
        s = jnp.where(allowed, s, NEG_FILL)
        s_scr[:, j * size:(j + 1) * size] = s
        top = jnp.maximum(top, jnp.max(s, axis=1, keepdims=True))
    total = jnp.zeros((size, 1), F32)
    for j in range(5):
        here = slice(j * size, (j + 1) * size)
        p = jnp.exp2((s_scr[:, here] - top) * (scaling * LOG2E))
        s_scr[:, here] = p
        total = total + jnp.sum(p, axis=1, keepdims=True)
    inverse = 1.0 / total
    out = jnp.zeros((size, DH), F32)
    for j in range(5):
        here = slice(j * size, (j + 1) * size)
        cols = slice((half + j) * size, (half + j + 1) * size)
        weight = s_scr[:, here] * inverse
        s_scr[:, here] = weight
        low = weight.astype(BF16)
        out = out + mm(low, v_ref[cols, :], NN)
        emit(1, half, j, mm(low, g, TN))
    o_ref[rows, :] = out.astype(BF16)
    row_dot = jnp.sum(g.astype(F32) * out, axis=1, keepdims=True)
    dq = jnp.zeros((size, DH), F32)
    for j in range(5):
        here = slice(j * size, (j + 1) * size)
        cols = slice((half + j) * size, (half + j + 1) * size)
        dp = mm(g, v_ref[cols, :], NT)
        ds = (s_scr[:, here] * (dp - row_dot)).astype(BF16)
        dq = dq + mm(ds, k_ref[cols, :], NN)
        emit(0, half, j, mm(ds, q, TN))
    dq_ref[rows, :] = (dq * scaling).astype(BF16)


def whole_kernel(blocks, width, heads, size,
                 k_in, v_in, q_in, g_in, t_in,
                 o_out, dq_out, dk_out, dv_out,
                 qt_ref, kwin, vwin, qs, gs, tw, lo, hi, o_st, dq_st, psend, prec, fin, center,
                 acc, s_scr,
                 in_send, in_recv, near_recv, in_local, t_send, t_recv, t_local,
                 halo_send, halo_recv, th_send, th_recv, part_send, part_recv,
                 out_send, out_recv, out_local):
    scaling = DH ** (-0.5)
    group = 2 * width
    seq = lax.axis_index("seq")
    head = lax.axis_index("head")
    blk = seq // 2
    me = (seq % 2) * width + head
    rows = k_in.shape[0]
    span = 2 * size
    has_low = blk > 0
    has_up = blk < blocks - 1
    mid = pl.ds(span, span)

    def peer(p):
        return (blk * 2 + p // width, p % width)

    low_dev = (seq - 2, head)
    up_dev = (seq + 2, head)

    def remote(src, dst, send, recv, dev):
        return pltpu.make_async_remote_copy(
            src_ref=src, dst_ref=dst, send_sem=send, recv_sem=recv, device_id=dev,
            device_id_type=pl.DeviceIdType.MESH)

    def each_peer(action):
        def step(d, carry):
            action((me + d) % group)
            return carry
        lax.fori_loop(1, group, step, 0)

    partner = me // 2 * 2 + (me + 1) % 2

    chips = group // 2
    chip = me // 2

    def each_far_chip(action):
        def step(d, carry):
            action((chip + d) % chips)
            return carry
        lax.fori_loop(1, chips, step, 0)

    def each_far(action):
        def both(c):
            action(c * 2)
            action(c * 2 + 1)
        each_far_chip(both)

    def wait_bytes(ref, sem):
        pltpu.make_async_copy(ref, ref, sem).wait()

    barrier = pltpu.get_barrier_semaphore()

    def greet(dev):
        pl.semaphore_signal(barrier, inc=1, device_id=dev, device_id_type=pl.DeviceIdType.MESH)

    each_peer(lambda p: greet(peer(p)))

    @pl.when(has_low)
    def _():
        greet(low_dev)

    @pl.when(has_up)
    def _():
        greet(up_dev)

    pl.semaphore_wait(barrier, group - 1 + has_low.astype(jnp.int32) + has_up.astype(jnp.int32))

    ins = (k_in, v_in, q_in, g_in)

    def landing(a, h, p):
        base = span if a < 2 else 0
        where = pl.ds(pl.multiple_of(base + p * rows, rows), rows)
        return (kwin, vwin, qs, gs)[a].at[h, where]

    def columns(p, h):
        return pl.ds(pl.multiple_of((p * heads + h) * DH, DH), DH)

    def spread(arrays, h):
        for a in arrays:
            pltpu.make_async_copy(ins[a].at[:, columns(me, h)], landing(a, h, me),
                                  in_local.at[a, h]).start()

        def send(p):
            for a in arrays:
                remote(ins[a].at[:, columns(p, h)], landing(a, h, me), in_send.at[a],
                       in_recv.at[a, h], peer(p)).start()
        if arrays[0] == 0:
            each_far(send)
        else:
            each_peer(send)

    def near(a, h):
        return remote(ins[a].at[:, columns(partner, h)], landing(a, h, me), in_send.at[a],
                      near_recv.at[a, h], peer(partner))

    def arrived(a, h):
        ref = (kwin, vwin, qs, gs)[a]
        wait_bytes(ref.at[h, pl.ds(0, (group - (2 if a < 2 else 1)) * rows)], in_recv.at[a, h])
        wait_bytes(ref.at[h, pl.ds(0, rows)], in_local.at[a, h])

    pltpu.make_async_copy(t_in, tw.at[group + me], t_local).start()
    each_peer(lambda p: remote(t_in, tw.at[group + me], t_send, t_recv, peer(p)).start())
    def halo_up(a, h):
        ref = (kwin, vwin)[a]
        return remote(ref.at[h, mid], ref.at[h, pl.ds(0, span)], halo_send.at[0, a, h],
                      halo_recv.at[0, a, h], up_dev)

    def halo_down(a, h):
        ref = (kwin, vwin)[a]
        return remote(ref.at[h, mid], ref.at[h, pl.ds(2 * span, span)], halo_send.at[1, a, h],
                      halo_recv.at[1, a, h], low_dev)

    def chunk(part, p):
        return pl.ds(pl.multiple_of(part * span + p * rows, rows), rows)

    def chunk_up(a, h, p, src):
        ref = (kwin, vwin)[a]

        @pl.when(has_up)
        def _():
            remote(src, ref.at[h, chunk(0, p)], halo_send.at[0, a, h], halo_recv.at[0, a, h],
                   up_dev).start()

    def chunk_down(a, h, p, src):
        ref = (kwin, vwin)[a]

        @pl.when(has_low)
        def _():
            remote(src, ref.at[h, chunk(2, p)], halo_send.at[1, a, h], halo_recv.at[1, a, h],
                   low_dev).start()

    def own_halo(h):
        for a in range(2):
            src = ins[a].at[:, columns(me, h)]
            chunk_up(a, h, me, src)
            chunk_down(a, h, me, src)

    for h in range(heads):
        for a in range(2):
            near(a, h).start()
    spread((0, 1), 0)
    for h in range(heads):
        own_halo(h)
    if heads > 1:
        spread((0, 1), 1)
    for h in range(heads):
        spread((2, 3), h)
        if h + 2 < heads:
            spread((0, 1), h + 2)

    def t_up():
        return remote(tw.at[pl.ds(group, group)], tw.at[pl.ds(0, group)], th_send.at[0],
                      th_recv.at[0], up_dev)

    def t_down():
        return remote(tw.at[pl.ds(group, group)], tw.at[pl.ds(2 * group, group)], th_send.at[1],
                      th_recv.at[1], low_dev)

    def pair(part, c):
        return pl.ds(pl.multiple_of(part * span + c * 2 * rows, 2 * rows), 2 * rows)

    def forward(h):
        for a in range(2):
            arrived(a, h)
            ref = (kwin, vwin)[a]

            def pass_on(c, a=a, ref=ref):
                src = ref.at[h, pair(1, c)]

                @pl.when(has_up)
                def _():
                    remote(src, ref.at[h, pair(0, c)], halo_send.at[0, a, h],
                           halo_recv.at[0, a, h], up_dev).start()

                @pl.when(has_low)
                def _():
                    remote(src, ref.at[h, pair(2, c)], halo_send.at[1, a, h],
                           halo_recv.at[1, a, h], low_dev).start()
            each_far_chip(pass_on)

    for h in range(heads):
        for a in range(2):
            near(a, h).wait_recv()
            src = (kwin, vwin)[a].at[h, chunk(1, partner)]
            chunk_up(a, h, partner, src)
            chunk_down(a, h, partner, src)

    @pl.when(jnp.logical_not(has_low))
    def _():
        kwin[:, 0:span, :] = jnp.zeros((heads, span, DH), BF16)
        vwin[:, 0:span, :] = jnp.zeros((heads, span, DH), BF16)
        tw[0:group] = jnp.full((group, 1, rows), -1, jnp.int32)

    @pl.when(jnp.logical_not(has_up))
    def _():
        kwin[:, 2 * span:3 * span, :] = jnp.zeros((heads, span, DH), BF16)
        vwin[:, 2 * span:3 * span, :] = jnp.zeros((heads, span, DH), BF16)
        tw[2 * group:3 * group] = jnp.full((group, 1, rows), -1, jnp.int32)

    place = lax.broadcasted_iota(jnp.int32, (size, 1), 0)
    offset = lax.div(place * SHARD_MS, jnp.full((size, 1), size, jnp.int32))
    qt_ref[0:size, :] = offset
    qt_ref[size:span, :] = offset + SHARD_MS

    wait_bytes(tw.at[pl.ds(0, group - 1)], t_recv)
    wait_bytes(tw.at[0], t_local)

    @pl.when(has_up)
    def _():
        t_up().start()

    @pl.when(has_low)
    def _():
        t_down().start()

    forward(0)
    if heads > 1:
        forward(1)

    @pl.when(has_low)
    def _():
        t_up().wait_recv()

    @pl.when(has_up)
    def _():
        t_down().wait_recv()

    first = blk * 2 * SHARD_MS
    for i in range(3 * group):
        t = tw[i]
        here = slice(i * rows, (i + 1) * rows)
        lo[:, here] = jnp.where(t >= 0, t - first, -FAR)
        hi[:, here] = jnp.where(t >= 0, t - first, FAR)

    outs = (o_out, dq_out, dk_out, dv_out)

    def piece(p):
        return pl.ds(pl.multiple_of(p * rows, rows), rows)

    def hand_back(i, src, h, p):
        @pl.when(p == me)
        def _():
            pltpu.make_async_copy(src.at[piece(me)], outs[i].at[:, columns(me, h)],
                                  out_local.at[i, h]).start()

        @pl.when(p != me)
        def _():
            remote(src.at[piece(p)], outs[i].at[:, columns(me, h)], out_send.at[i],
                   out_recv.at[i], peer(p)).start()

    def collect(half, h):
        for i, src in enumerate((o_st, dq_st)):
            def step(d, carry, i=i, src=src):
                hand_back(i, src.at[h], h, half * width + (head + d) % width)
                return carry
            lax.fori_loop(0, width, step, 0)

    def both_pieces(c):
        return pl.ds(pl.multiple_of(c * 2 * rows, 2 * rows), 2 * rows)

    def part_down(a, h, c):
        return remote(psend.at[0, a, h, both_pieces(c)], prec.at[0, a, h, both_pieces(c)],
                      part_send.at[0, a, h], part_recv.at[0, a, h, c], low_dev)

    def part_up(a, h, c):
        return remote(psend.at[1, a, h, both_pieces(c)], prec.at[1, a, h, both_pieces(c)],
                      part_send.at[1, a, h], part_recv.at[1, a, h, c], up_dev)

    def early_parts(h):
        @pl.when(has_low)
        def _():
            for a in (1, 0):
                for c in range(chips // 2):
                    part_down(a, h, c).start()

    def late_parts(h):
        for a in (1, 0):
            @pl.when(has_low)
            def _(a=a):
                for c in range(chips // 2, chips):
                    part_down(a, h, c).start()

            @pl.when(has_up)
            def _(a=a):
                each_far_chip(lambda c: part_up(a, h, c).start())
                part_up(a, h, chip).start()

    def finish(h):
        for a in (1, 0):
            def add(c, a=a):
                here = both_pieces(c)

                @pl.when(has_up)
                def _():
                    part_down(a, h, c).wait_recv()
                    center[a, h, here] = center[a, h, here] + prec[0, a, h, here].astype(F32)

                @pl.when(has_low)
                def _():
                    part_up(a, h, c).wait_recv()
                    center[a, h, here] = center[a, h, here] + prec[1, a, h, here].astype(F32)

                fin[a, h, here] = center[a, h, here].astype(BF16)

            def send(p, a=a):
                remote(fin.at[a, h, piece(p)], outs[2 + a].at[:, columns(me, h)],
                       out_send.at[2 + a], out_recv.at[2 + a], peer(p)).start()

            def one(c, a=a):
                add(c)
                send(c * 2)
                send(c * 2 + 1)
            each_far_chip(one)
            add(chip)
            send(partner)
            pltpu.make_async_copy(fin.at[a, h, piece(me)], outs[2 + a].at[:, columns(me, h)],
                                  out_local.at[2 + a, h]).start()

    def one_head(h, carry):
        for a in range(2):
            @pl.when(has_low)
            def _(a=a):
                halo_up(a, h).wait_recv()

            @pl.when(has_up)
            def _(a=a):
                halo_down(a, h).wait_recv()
        arrived(2, h)
        arrived(3, h)

        def emit(a, half, j, x):
            spot = half + j
            if half == 0 and j > 0:
                acc[a, (j - 1) * size:j * size, :] = x
                return
            if half == 1 and j < 4:
                x = acc[a, j * size:(j + 1) * size, :] + x
            if a == 0:
                x = x * scaling
            there = slice(spot % 2 * size, (spot % 2 + 1) * size)
            if spot // 2 == 1:
                center[a, h, there] = x
            else:
                psend[spot // 4, a, h, there] = x.astype(BF16)

        refs = (size, qs.at[h], gs.at[h], kwin.at[h], vwin.at[h], qt_ref, lo, hi,
                o_st.at[h], dq_st.at[h], emit, s_scr)
        attend_half(0, *refs)
        collect(0, h)

        @pl.when(h + 2 < heads)
        def _():
            forward(h + 2)

        early_parts(h)

        @pl.when(h >= 2)
        def _():
            finish(h - 2)

        attend_half(1, *refs)
        late_parts(h)
        collect(1, h)
        return carry

    lax.fori_loop(0, heads, one_head, 0)

    def settle(h, carry):
        finish(h)
        return carry

    lax.fori_loop(max(heads - 2, 0), heads, settle, 0)

    sent = (group - 1) * heads * DH
    wait_bytes(tw.at[pl.ds(0, group - 1)], t_send)
    for a in range(4):
        wait_bytes(ins[a].at[:, pl.ds(0, sent)], in_send.at[a])
        wait_bytes(outs[a].at[:, pl.ds(0, sent)], out_send.at[a])
        wait_bytes(outs[a].at[:, pl.ds(0, sent)], out_recv.at[a])
        for h in range(heads):
            wait_bytes(outs[a].at[:, pl.ds(0, DH)], out_local.at[a, h])

    @pl.when(has_up)
    def _():
        t_up().wait_send()
        for a in range(2):
            for h in range(heads):
                halo_up(a, h).wait_send()
                wait_bytes(psend.at[1, a, h], part_send.at[1, a, h])

    @pl.when(has_low)
    def _():
        t_down().wait_send()
        for a in range(2):
            for h in range(heads):
                halo_down(a, h).wait_send()
                wait_bytes(psend.at[0, a, h], part_send.at[0, a, h])


def hand_over(*refs):
    srcs, dsts, sem = refs[:4], refs[4:8], refs[8]
    stores = [pltpu.make_async_copy(srcs[i], dsts[i], sem.at[i]) for i in range(4)]
    for store in stores:
        store.start()
    for store in stores:
        store.wait()


def on_device(seq_count, head_count, video_query, audio_key, audio_value, grad_out, audio_time):
    group = 2 * head_count
    rows, features = video_query.shape
    size = rows * head_count
    span = 2 * size
    heads = features // DH // group
    hbm = pl.BlockSpec(memory_space=pl.ANY)
    vmem = pl.BlockSpec(memory_space=pltpu.VMEM)
    dma = pltpu.SemaphoreType.DMA
    pairs = heads * span * 5 * size
    o, dq, dk, dv = pl.pallas_call(
        functools.partial(whole_kernel, seq_count // 2, head_count, heads, size),
        in_specs=[pl.BlockSpec(memory_space=pltpu.HBM)] * 5,
        out_specs=[vmem] * 4,
        out_shape=[pltpu.VMEM((rows, features), BF16)] * 4,
        scratch_shapes=[
            pltpu.VMEM((span, 1), jnp.int32),
            pltpu.VMEM((heads, 3 * span, DH), BF16),
            pltpu.VMEM((heads, 3 * span, DH), BF16),
            pltpu.VMEM((heads, span, DH), BF16),
            pltpu.VMEM((heads, span, DH), BF16),
            pltpu.VMEM((3 * group, 1, rows), jnp.int32),
            pltpu.VMEM((1, 3 * span), jnp.int32),
            pltpu.VMEM((1, 3 * span), jnp.int32),
            pltpu.VMEM((heads, span, DH), BF16),
            pltpu.VMEM((heads, span, DH), BF16),
            pltpu.VMEM((2, 2, heads, span, DH), BF16),
            pltpu.VMEM((2, 2, heads, span, DH), BF16),
            pltpu.VMEM((2, heads, span, DH), BF16),
            pltpu.VMEM((2, heads, span, DH), F32),
            pltpu.VMEM((2, 4 * size, DH), F32),
            pltpu.VMEM((size, 5 * size), F32),
            dma((4,)), dma((4, heads)), dma((2, heads)), dma((4, heads)), dma, dma, dma,
            dma((2, 2, heads)), dma((2, 2, heads)), dma((2,)), dma((2,)),
            dma((2, 2, heads)), dma((2, 2, heads, head_count)),
            dma((4,)), dma((4,)), dma((4, heads)),
        ],
        compiler_params=pltpu.CompilerParams(
            collective_id=0, has_side_effects=True, vmem_limit_bytes=52 * 1024 * 1024),
        cost_estimate=pl.CostEstimate(flops=12 * pairs * DH, bytes_accessed=16 * rows * features,
                                      transcendentals=pairs),
    )(audio_key, audio_value, video_query, grad_out, audio_time[None, :])
    return pl.pallas_call(
        hand_over, in_specs=[hbm] * 4, out_specs=[hbm] * 4,
        out_shape=[jax.ShapeDtypeStruct((rows, features), BF16)] * 4,
        scratch_shapes=[dma((4,))],
        compiler_params=pltpu.CompilerParams(vmem_limit_bytes=4 * 1024 * 1024),
    )(o, dq, dk, dv)


def solution(mesh):
    rows = P(("seq", "head"), None)
    return jax.shard_map(
        functools.partial(on_device, mesh.shape["seq"], mesh.shape["head"]),
        mesh=mesh,
        in_specs=(rows, rows, rows, rows, P(("seq", "head"))),
        out_specs=(rows, rows, rows, rows),
        check_vma=False,
    )
```

```python
import functools

import jax
import jax.numpy as jnp
from jax import lax
from jax.experimental import pallas as pl
from jax.experimental.pallas import tpu as pltpu
from jax.sharding import PartitionSpec as P

DH = 128
SHARD_MS = 625
RADIUS_MS = 1000
NEG_FILL = -1e30
FAR = 1 << 30
LOG2E = 1.4426950408889634
F32 = jnp.float32
BF16 = jnp.bfloat16
NT = (((1,), (1,)), ((), ()))
NN = (((1,), (0,)), ((), ()))
TN = (((0,), (0,)), ((), ()))


def mm(a, b, dims):
    return lax.dot_general(a, b, dims, preferred_element_type=F32)


def attend_half(half, size, q_ref, g_ref, k_ref, v_ref, qt_ref, lo_ref, hi_ref, o_ref,
                dq_ref, emit, s_scr):
    scaling = DH ** (-0.5)
    rows = slice(half * size, (half + 1) * size)
    q = q_ref[rows, :]
    g = g_ref[rows, :]
    stamp = qt_ref[rows, :]
    top = jnp.full((size, 1), -jnp.inf, F32)
    for j in range(5):
        cols = slice((half + j) * size, (half + j + 1) * size)
        s = mm(q, k_ref[cols, :], NT)
        if j <= 2:
            allowed = lo_ref[:, cols] >= stamp - RADIUS_MS
        else:
            allowed = hi_ref[:, cols] <= stamp + RADIUS_MS
        s = jnp.where(allowed, s, NEG_FILL)
        s_scr[:, j * size:(j + 1) * size] = s
        top = jnp.maximum(top, jnp.max(s, axis=1, keepdims=True))
    total = jnp.zeros((size, 1), F32)
    for j in range(5):
        here = slice(j * size, (j + 1) * size)
        p = jnp.exp2((s_scr[:, here] - top) * (scaling * LOG2E))
        s_scr[:, here] = p
        total = total + jnp.sum(p, axis=1, keepdims=True)
    inverse = 1.0 / total
    out = jnp.zeros((size, DH), F32)
    for j in range(5):
        here = slice(j * size, (j + 1) * size)
        cols = slice((half + j) * size, (half + j + 1) * size)
        weight = s_scr[:, here] * inverse
        s_scr[:, here] = weight
        low = weight.astype(BF16)
        out = out + mm(low, v_ref[cols, :], NN)
        emit(1, half, j, mm(low, g, TN))
    o_ref[rows, :] = out.astype(BF16)
    row_dot = jnp.sum(g.astype(F32) * out, axis=1, keepdims=True)
    dq = jnp.zeros((size, DH), F32)
    for j in range(5):
        here = slice(j * size, (j + 1) * size)
        cols = slice((half + j) * size, (half + j + 1) * size)
        dp = mm(g, v_ref[cols, :], NT)
        ds = (s_scr[:, here] * (dp - row_dot)).astype(BF16)
        dq = dq + mm(ds, k_ref[cols, :], NN)
        emit(0, half, j, mm(ds, q, TN))
    dq_ref[rows, :] = (dq * scaling).astype(BF16)


def whole_kernel(blocks, width, heads, size,
                 k_in, v_in, q_in, g_in, t_in,
                 o_out, dq_out, dk_out, dv_out,
                 qt_ref, kwin, vwin, qs, gs, tw, lo, hi, o_st, dq_st, psend, prec, fin, center,
                 acc, s_scr,
                 in_send, in_recv, near_recv, in_local, t_send, t_recv, t_local,
                 halo_send, halo_recv, th_send, th_recv, part_send, part_recv,
                 out_send, out_recv, out_local):
    scaling = DH ** (-0.5)
    group = 2 * width
    seq = lax.axis_index("seq")
    head = lax.axis_index("head")
    blk = seq // 2
    me = (seq % 2) * width + head
    rows = k_in.shape[0]
    span = 2 * size
    has_low = blk > 0
    has_up = blk < blocks - 1
    mid = pl.ds(span, span)

    def peer(p):
        return (blk * 2 + p // width, p % width)

    low_dev = (seq - 2, head)
    up_dev = (seq + 2, head)

    def remote(src, dst, send, recv, dev):
        return pltpu.make_async_remote_copy(
            src_ref=src, dst_ref=dst, send_sem=send, recv_sem=recv, device_id=dev,
            device_id_type=pl.DeviceIdType.MESH)

    def each_peer(action):
        def step(d, carry):
            action((me + d) % group)
            return carry
        lax.fori_loop(1, group, step, 0)

    partner = me // 2 * 2 + (me + 1) % 2

    chips = group // 2
    chip = me // 2

    def each_far_chip(action):
        def step(d, carry):
            action((chip + d) % chips)
            return carry
        lax.fori_loop(1, chips, step, 0)

    def each_far(action):
        def both(c):
            action(c * 2)
            action(c * 2 + 1)
        each_far_chip(both)

    def wait_bytes(ref, sem):
        pltpu.make_async_copy(ref, ref, sem).wait()

    barrier = pltpu.get_barrier_semaphore()

    def greet(dev):
        pl.semaphore_signal(barrier, inc=1, device_id=dev, device_id_type=pl.DeviceIdType.MESH)

    each_peer(lambda p: greet(peer(p)))

    @pl.when(has_low)
    def _():
        greet(low_dev)

    @pl.when(has_up)
    def _():
        greet(up_dev)

    pl.semaphore_wait(barrier, group - 1 + has_low.astype(jnp.int32) + has_up.astype(jnp.int32))

    ins = (k_in, v_in, q_in, g_in)

    def landing(a, h, p):
        base = span if a < 2 else 0
        where = pl.ds(pl.multiple_of(base + p * rows, rows), rows)
        return (kwin, vwin, qs, gs)[a].at[h, where]

    def columns(p, h):
        return pl.ds(pl.multiple_of((p * heads + h) * DH, DH), DH)

    def spread(arrays, h):
        for a in arrays:
            pltpu.make_async_copy(ins[a].at[:, columns(me, h)], landing(a, h, me),
                                  in_local.at[a, h]).start()

        def send(p):
            for a in arrays:
                remote(ins[a].at[:, columns(p, h)], landing(a, h, me), in_send.at[a],
                       in_recv.at[a, h], peer(p)).start()
        if arrays[0] == 0:
            each_far(send)
        else:
            each_peer(send)

    def near(a, h):
        return remote(ins[a].at[:, columns(partner, h)], landing(a, h, me), in_send.at[a],
                      near_recv.at[a, h], peer(partner))

    def arrived(a, h):
        ref = (kwin, vwin, qs, gs)[a]
        wait_bytes(ref.at[h, pl.ds(0, (group - (2 if a < 2 else 1)) * rows)], in_recv.at[a, h])
        wait_bytes(ref.at[h, pl.ds(0, rows)], in_local.at[a, h])

    pltpu.make_async_copy(t_in, tw.at[group + me], t_local).start()
    each_peer(lambda p: remote(t_in, tw.at[group + me], t_send, t_recv, peer(p)).start())
    def halo_up(a, h):
        ref = (kwin, vwin)[a]
        return remote(ref.at[h, mid], ref.at[h, pl.ds(0, span)], halo_send.at[0, a, h],
                      halo_recv.at[0, a, h], up_dev)

    def halo_down(a, h):
        ref = (kwin, vwin)[a]
        return remote(ref.at[h, mid], ref.at[h, pl.ds(2 * span, span)], halo_send.at[1, a, h],
                      halo_recv.at[1, a, h], low_dev)

    def chunk(part, p):
        return pl.ds(pl.multiple_of(part * span + p * rows, rows), rows)

    def chunk_up(a, h, p, src):
        ref = (kwin, vwin)[a]

        @pl.when(has_up)
        def _():
            remote(src, ref.at[h, chunk(0, p)], halo_send.at[0, a, h], halo_recv.at[0, a, h],
                   up_dev).start()

    def chunk_down(a, h, p, src):
        ref = (kwin, vwin)[a]

        @pl.when(has_low)
        def _():
            remote(src, ref.at[h, chunk(2, p)], halo_send.at[1, a, h], halo_recv.at[1, a, h],
                   low_dev).start()

    def own_halo(h):
        for a in range(2):
            src = ins[a].at[:, columns(me, h)]
            chunk_up(a, h, me, src)
            chunk_down(a, h, me, src)

    for h in range(heads):
        for a in range(2):
            near(a, h).start()
    spread((0, 1), 0)
    for h in range(heads):
        own_halo(h)
    if heads > 1:
        spread((0, 1), 1)
    for h in range(heads):
        spread((2, 3), h)
        if h + 2 < heads:
            spread((0, 1), h + 2)

    def t_up():
        return remote(tw.at[pl.ds(group, group)], tw.at[pl.ds(0, group)], th_send.at[0],
                      th_recv.at[0], up_dev)

    def t_down():
        return remote(tw.at[pl.ds(group, group)], tw.at[pl.ds(2 * group, group)], th_send.at[1],
                      th_recv.at[1], low_dev)

    def pair(part, c):
        return pl.ds(pl.multiple_of(part * span + c * 2 * rows, 2 * rows), 2 * rows)

    def forward(h):
        for a in range(2):
            arrived(a, h)
            ref = (kwin, vwin)[a]

            def pass_on(c, a=a, ref=ref):
                src = ref.at[h, pair(1, c)]

                @pl.when(has_up)
                def _():
                    remote(src, ref.at[h, pair(0, c)], halo_send.at[0, a, h],
                           halo_recv.at[0, a, h], up_dev).start()

                @pl.when(has_low)
                def _():
                    remote(src, ref.at[h, pair(2, c)], halo_send.at[1, a, h],
                           halo_recv.at[1, a, h], low_dev).start()
            each_far_chip(pass_on)

    for h in range(heads):
        for a in range(2):
            near(a, h).wait_recv()
            src = (kwin, vwin)[a].at[h, chunk(1, partner)]
            chunk_up(a, h, partner, src)
            chunk_down(a, h, partner, src)

    @pl.when(jnp.logical_not(has_low))
    def _():
        kwin[:, 0:span, :] = jnp.zeros((heads, span, DH), BF16)
        vwin[:, 0:span, :] = jnp.zeros((heads, span, DH), BF16)
        tw[0:group] = jnp.full((group, 1, rows), -1, jnp.int32)

    @pl.when(jnp.logical_not(has_up))
    def _():
        kwin[:, 2 * span:3 * span, :] = jnp.zeros((heads, span, DH), BF16)
        vwin[:, 2 * span:3 * span, :] = jnp.zeros((heads, span, DH), BF16)
        tw[2 * group:3 * group] = jnp.full((group, 1, rows), -1, jnp.int32)

    place = lax.broadcasted_iota(jnp.int32, (size, 1), 0)
    offset = lax.div(place * SHARD_MS, jnp.full((size, 1), size, jnp.int32))
    qt_ref[0:size, :] = offset
    qt_ref[size:span, :] = offset + SHARD_MS

    wait_bytes(tw.at[pl.ds(0, group - 1)], t_recv)
    wait_bytes(tw.at[0], t_local)

    @pl.when(has_up)
    def _():
        t_up().start()

    @pl.when(has_low)
    def _():
        t_down().start()

    forward(0)
    if heads > 1:
        forward(1)

    @pl.when(has_low)
    def _():
        t_up().wait_recv()

    @pl.when(has_up)
    def _():
        t_down().wait_recv()

    first = blk * 2 * SHARD_MS
    for i in range(3 * group):
        t = tw[i]
        here = slice(i * rows, (i + 1) * rows)
        lo[:, here] = jnp.where(t >= 0, t - first, -FAR)
        hi[:, here] = jnp.where(t >= 0, t - first, FAR)

    outs = (o_out, dq_out, dk_out, dv_out)

    def piece(p):
        return pl.ds(pl.multiple_of(p * rows, rows), rows)

    def hand_back(i, src, h, p):
        @pl.when(p == me)
        def _():
            pltpu.make_async_copy(src.at[piece(me)], outs[i].at[:, columns(me, h)],
                                  out_local.at[i, h]).start()

        @pl.when(p != me)
        def _():
            remote(src.at[piece(p)], outs[i].at[:, columns(me, h)], out_send.at[i],
                   out_recv.at[i], peer(p)).start()

    def collect(half, h):
        for i, src in enumerate((o_st, dq_st)):
            def step(d, carry, i=i, src=src):
                hand_back(i, src.at[h], h, half * width + (head + d) % width)
                return carry
            lax.fori_loop(0, width, step, 0)

    def both_pieces(c):
        return pl.ds(pl.multiple_of(c * 2 * rows, 2 * rows), 2 * rows)

    def part_down(a, h, c):
        return remote(psend.at[0, a, h, both_pieces(c)], prec.at[0, a, h, both_pieces(c)],
                      part_send.at[0, a, h], part_recv.at[0, a, h, c], low_dev)

    def part_up(a, h, c):
        return remote(psend.at[1, a, h, both_pieces(c)], prec.at[1, a, h, both_pieces(c)],
                      part_send.at[1, a, h], part_recv.at[1, a, h, c], up_dev)

    def send_parts(h):
        for a in (1, 0):
            @pl.when(has_low)
            def _(a=a):
                each_far_chip(lambda c: part_down(a, h, c).start())
                part_down(a, h, chip).start()

            @pl.when(has_up)
            def _(a=a):
                each_far_chip(lambda c: part_up(a, h, c).start())
                part_up(a, h, chip).start()

    def finish(h):
        for a in (1, 0):
            def add(c, a=a):
                here = both_pieces(c)

                @pl.when(has_up)
                def _():
                    part_down(a, h, c).wait_recv()
                    center[a, h, here] = center[a, h, here] + prec[0, a, h, here].astype(F32)

                @pl.when(has_low)
                def _():
                    part_up(a, h, c).wait_recv()
                    center[a, h, here] = center[a, h, here] + prec[1, a, h, here].astype(F32)

                fin[a, h, here] = center[a, h, here].astype(BF16)

            def send(p, a=a):
                remote(fin.at[a, h, piece(p)], outs[2 + a].at[:, columns(me, h)],
                       out_send.at[2 + a], out_recv.at[2 + a], peer(p)).start()

            def one(c, a=a):
                add(c)
                send(c * 2)
                send(c * 2 + 1)
            each_far_chip(one)
            add(chip)
            send(partner)
            pltpu.make_async_copy(fin.at[a, h, piece(me)], outs[2 + a].at[:, columns(me, h)],
                                  out_local.at[2 + a, h]).start()

    def one_head(h, carry):
        for a in range(2):
            @pl.when(has_low)
            def _(a=a):
                halo_up(a, h).wait_recv()

            @pl.when(has_up)
            def _(a=a):
                halo_down(a, h).wait_recv()
        arrived(2, h)
        arrived(3, h)

        def emit(a, half, j, x):
            spot = half + j
            if half == 0 and j > 0:
                acc[a, (j - 1) * size:j * size, :] = x
                return
            if half == 1 and j < 4:
                x = acc[a, j * size:(j + 1) * size, :] + x
            if a == 0:
                x = x * scaling
            there = slice(spot % 2 * size, (spot % 2 + 1) * size)
            if spot // 2 == 1:
                center[a, h, there] = x
            else:
                psend[spot // 4, a, h, there] = x.astype(BF16)

        refs = (size, qs.at[h], gs.at[h], kwin.at[h], vwin.at[h], qt_ref, lo, hi,
                o_st.at[h], dq_st.at[h], emit, s_scr)
        attend_half(0, *refs)
        collect(0, h)

        @pl.when(h + 2 < heads)
        def _():
            forward(h + 2)

        @pl.when(h >= 2)
        def _():
            finish(h - 2)

        attend_half(1, *refs)
        send_parts(h)
        collect(1, h)
        return carry

    lax.fori_loop(0, heads, one_head, 0)

    def settle(h, carry):
        finish(h)
        return carry

    lax.fori_loop(max(heads - 2, 0), heads, settle, 0)

    sent = (group - 1) * heads * DH
    wait_bytes(tw.at[pl.ds(0, group - 1)], t_send)
    for a in range(4):
        wait_bytes(ins[a].at[:, pl.ds(0, sent)], in_send.at[a])
        wait_bytes(outs[a].at[:, pl.ds(0, sent)], out_send.at[a])
        wait_bytes(outs[a].at[:, pl.ds(0, sent)], out_recv.at[a])
        for h in range(heads):
            wait_bytes(outs[a].at[:, pl.ds(0, DH)], out_local.at[a, h])

    @pl.when(has_up)
    def _():
        t_up().wait_send()
        for a in range(2):
            for h in range(heads):
                halo_up(a, h).wait_send()
                wait_bytes(psend.at[1, a, h], part_send.at[1, a, h])

    @pl.when(has_low)
    def _():
        t_down().wait_send()
        for a in range(2):
            for h in range(heads):
                halo_down(a, h).wait_send()
                wait_bytes(psend.at[0, a, h], part_send.at[0, a, h])


def hand_over(*refs):
    srcs, dsts, sem = refs[:4], refs[4:8], refs[8]
    stores = [pltpu.make_async_copy(srcs[i], dsts[i], sem.at[i]) for i in range(4)]
    for store in stores:
        store.start()
    for store in stores:
        store.wait()


def on_device(seq_count, head_count, video_query, audio_key, audio_value, grad_out, audio_time):
    group = 2 * head_count
    rows, features = video_query.shape
    size = rows * head_count
    span = 2 * size
    heads = features // DH // group
    hbm = pl.BlockSpec(memory_space=pl.ANY)
    vmem = pl.BlockSpec(memory_space=pltpu.VMEM)
    dma = pltpu.SemaphoreType.DMA
    pairs = heads * span * 5 * size
    o, dq, dk, dv = pl.pallas_call(
        functools.partial(whole_kernel, seq_count // 2, head_count, heads, size),
        in_specs=[pl.BlockSpec(memory_space=pltpu.HBM)] * 5,
        out_specs=[vmem] * 4,
        out_shape=[pltpu.VMEM((rows, features), BF16)] * 4,
        scratch_shapes=[
            pltpu.VMEM((span, 1), jnp.int32),
            pltpu.VMEM((heads, 3 * span, DH), BF16),
            pltpu.VMEM((heads, 3 * span, DH), BF16),
            pltpu.VMEM((heads, span, DH), BF16),
            pltpu.VMEM((heads, span, DH), BF16),
            pltpu.VMEM((3 * group, 1, rows), jnp.int32),
            pltpu.VMEM((1, 3 * span), jnp.int32),
            pltpu.VMEM((1, 3 * span), jnp.int32),
            pltpu.VMEM((heads, span, DH), BF16),
            pltpu.VMEM((heads, span, DH), BF16),
            pltpu.VMEM((2, 2, heads, span, DH), BF16),
            pltpu.VMEM((2, 2, heads, span, DH), BF16),
            pltpu.VMEM((2, heads, span, DH), BF16),
            pltpu.VMEM((2, heads, span, DH), F32),
            pltpu.VMEM((2, 4 * size, DH), F32),
            pltpu.VMEM((size, 5 * size), F32),
            dma((4,)), dma((4, heads)), dma((2, heads)), dma((4, heads)), dma, dma, dma,
            dma((2, 2, heads)), dma((2, 2, heads)), dma((2,)), dma((2,)),
            dma((2, 2, heads)), dma((2, 2, heads, head_count)),
            dma((4,)), dma((4,)), dma((4, heads)),
        ],
        compiler_params=pltpu.CompilerParams(
            collective_id=0, has_side_effects=True, vmem_limit_bytes=52 * 1024 * 1024),
        cost_estimate=pl.CostEstimate(flops=12 * pairs * DH, bytes_accessed=16 * rows * features,
                                      transcendentals=pairs),
    )(audio_key, audio_value, video_query, grad_out, audio_time[None, :])
    return pl.pallas_call(
        hand_over, in_specs=[hbm] * 4, out_specs=[hbm] * 4,
        out_shape=[jax.ShapeDtypeStruct((rows, features), BF16)] * 4,
        scratch_shapes=[dma((4,))],
        compiler_params=pltpu.CompilerParams(vmem_limit_bytes=4 * 1024 * 1024),
    )(o, dq, dk, dv)


def solution(mesh):
    rows = P(("seq", "head"), None)
    return jax.shard_map(
        functools.partial(on_device, mesh.shape["seq"], mesh.shape["head"]),
        mesh=mesh,
        in_specs=(rows, rows, rows, rows, P(("seq", "head"))),
        out_specs=(rows, rows, rows, rows),
        check_vma=False,
    )
```
